32 devices in a mesh: corpus: 4 (over z), rerank: 8 (over y, x, core).
Axes of the slice: x: 2, y: 2, z: 4, core: 2. Of those that a mesh axis runs over, the one named last changes fastest.
Arguments:
- store_rows: bfloat16 [128, 512, 3584], P('corpus', 'rerank'), may hold values from -400 to 400
- block_lengths: int32 [128], replicated, may hold values from 128 to 512
- queries: bfloat16 [32, 64, 3584], P(None, 'rerank'), may hold values from -400 to 400
- cand_owner: int32 [64, 1], replicated, may hold values from 0 to 3; in each aligned block of 16 rows (0 to 15, 16 to 31, ...) at most 5 rows name the same one
- cand_block: int32 [64], replicated, may hold values from 0 to 31
- cand_query: int32 [64], replicated, may hold values from 0 to 31
- norm_gain: bfloat16 [3584], replicated, may hold values from 0.099609375 to 1.8984375
- w_query: bfloat16 [3584, 1792], P('rerank'), may hold values from -8 to 8
- w_key: bfloat16 [3584, 256], P('rerank'), may hold values from -1 to 1
- w_value: bfloat16 [3584, 256], P('rerank'), may hold values from -0.09375 to 0.09375
- w_score: bfloat16 [1792], replicated, may hold values from -0.125 to 0.125
Outputs:
- passage_context: bfloat16 [80, 512, 1792], P('corpus', 'rerank')
- pair_scores: float32 [64], P(('corpus', 'rerank'))
The draws below stay inside these ranges and needn't reach their ends.
Inputs may be any that keep to these rules, and one draw needn't show every extreme that they name: `cand_owner`: at most 5 of the 16 pairs of one corpus group (an aligned block of rows) name the same owner, in every draw, some group names one owner in exactly 5 of its 16 pairs.
All inputs are finite; a program needn't handle non-finite values.
Results may differ from the reference program's by a relative error of at most 0.013.
Values may be sent and summed in bfloat16 or wider, within the bound.
A program may use at most 128 MiB of HBM per device.

```python
import math
import jax
import jax.numpy as jnp
import numpy as np
from jax import lax

D = 3584
HDIM = 128
QHEADS = 14
KVHEADS = 2
QW = 1792
KW = 256
BLK = 512
QLEN = 64
CAP = 5
PAIR_C = 16
PAIRS = 64
OWN_BLKS = 32
NQ = 32
BLOCKS = 128
N_CORPUS = 4


def hidden_rows(key, shape):
    noise_key = jax.random.fold_in(key, 3)
    column_key = jax.random.fold_in(key, 5)
    row_key = jax.random.fold_in(key, 7)
    base = jax.random.truncated_normal(noise_key, -4.0, 4.0, shape, jnp.float32)
    columns = jnp.exp(jax.random.uniform(column_key, (shape[-1],), jnp.float32, 0.0, math.log(10.0)))
    row_scale = jnp.exp(jax.random.uniform(row_key, shape[:-1] + (1,), jnp.float32, 0.0, math.log(10.0)))
    return jnp.clip(base * columns * row_scale, -400.0, 400.0)


def draw_store_rows(key, part):
    return hidden_rows(jax.random.fold_in(key, 101), (BLOCKS, BLK, D)).astype(jnp.bfloat16)


def draw_queries(key, part):
    return hidden_rows(jax.random.fold_in(key, 202), (NQ, QLEN, D)).astype(jnp.bfloat16)


def key_matrix(key):
    return jax.random.truncated_normal(jax.random.fold_in(key, 11), -4.0, 4.0, (D, KVHEADS * HDIM), jnp.float32) * D ** (-0.5)


def draw_w_key(key, part):
    return key_matrix(key).astype(jnp.bfloat16)


def draw_w_query(key, part):
    noise = jax.random.truncated_normal(jax.random.fold_in(key, 23), -4.0, 4.0, (D, QHEADS * HDIM), jnp.float32) * D ** (-0.5)
    return noise.astype(jnp.bfloat16)


def plant(array, rng, least, high):
    spot = [jax.random.randint(jax.random.fold_in(rng, axis), (), 0, length) for axis, length in enumerate(array.shape)]
    widest = array.shape.index(max(array.shape))
    beside = spot[:widest] + [(spot[widest] + 1) % array.shape[widest]] + spot[widest + 1:]
    return array.at[tuple(spot)].set(least).at[tuple(beside)].set(high)


def block_levels(own_key, dims, cuts, smallest, largest):
    def one(position, blocks):
        heights = jax.random.uniform(jax.random.fold_in(jax.random.fold_in(own_key, 6), position), (blocks,), jnp.float32, smallest / len(cuts), largest / len(cuts))
        return jnp.repeat(jnp.exp(heights), dims[position] // blocks).reshape((-1,) + (1,) * (len(dims) - position - 1))

    factor_of = one(*cuts[0])
    for cut in cuts[1:]:
        factor_of = factor_of * one(*cut)
    return factor_of


def deal_out(own_key, own, number, rows, count, top, bound, slope):
    ranking = jax.random.permutation(own_key, count)
    heavy_load, usual = load_shares(count, rows * top, bound, slope, True), load_shares(count, rows * top, bound, slope, False)
    places = jnp.arange(count)

    def named(lengths, turn):
        used = int((lengths > 0).sum())
        fixed = max(1, used // 4)
        passed = fixed + (places - fixed + turn * (used - fixed)) % max(1, count - fixed)
        return jnp.zeros((count,), jnp.int32).at[ranking[jnp.where(places < fixed, places, passed)]].set(jnp.asarray(lengths, jnp.int32))

    lengths = jnp.where(number % 4 == 0, named(heavy_load, number // 4), named(usual, number - number // 4 - 1))
    mixed = jax.random.permutation(jax.random.fold_in(own, 3), count)
    donor, taker = mixed[0:count // 2 * 2:2], mixed[1:count // 2 * 2:2]
    margin = jnp.minimum(lengths[donor] - 1, bound - lengths[taker]) // 2
    margin = jnp.where((donor == ranking[0]) | (taker == ranking[0]) | (lengths[taker] == 0), 0, jnp.maximum(margin, 0))
    passed = jax.random.randint(jax.random.fold_in(own, 4), (count // 2,), 0, 1 << 20) % (margin + 1)
    lengths = lengths.at[donor].add(-passed).at[taker].add(passed)
    labels = jnp.searchsorted(jnp.cumsum(lengths), jnp.arange(rows * top), side="right").astype(jnp.int32)
    listing = labels.reshape(top, rows).T
    listing = listing[jax.random.permutation(jax.random.fold_in(own, 1), rows)]
    turn = jax.random.randint(jax.random.fold_in(own, 2), (rows, 1), 0, top)
    return jnp.take_along_axis(listing, (jnp.arange(top)[None, :] + turn) % top, axis=1)


def load_shares(number_of, total, reach, lean, full):
    loads = [(1 << 20) // math.isqrt(standing ** lean) + 1 for standing in range(1, number_of + 1)]
    largest = reach if full else min(reach, max(-(-total // number_of), total * loads[0] // sum(loads)))
    least = 1 if total - largest >= number_of - 1 else 0
    counts, rest = [largest] + [least] * (number_of - 1), total - largest - least * (number_of - 1)
    while rest > 0:
        free = [i for i in range(1, number_of) if counts[i] < largest] or [i for i in range(1, number_of) if counts[i] < reach]
        mass, budget = sum([loads[i] for i in free]), rest
        for i in free:
            addition = min(reach - counts[i], max(1, budget * loads[i] // mass), rest)
            counts[i] = counts[i] + addition
            rest = rest - addition
    return np.array(counts)


def gaussian(key, dims, deviation, reach, split=(), kind=jnp.bfloat16):
    result = jax.random.normal(key, dims, jnp.float32) * deviation
    if len(split) > 0:
        result = block_levels(key, dims, split, -0.22, 0.18) * result
    return jnp.clip(result, min=-reach, max=reach).astype(kind)


def setup_inputs(seed: int = 0) -> dict:
    seeds = jax.random.split(jax.random.key(seed), 12)
    store_rows = draw_store_rows(jax.random.fold_in(seeds[11], 71), 0)
    block_lengths = plant(jax.random.randint(seeds[1], (BLOCKS,), BLK // 4, BLK + 1), jax.random.fold_in(seeds[1], 1), BLK // 4, BLK).astype(jnp.int32)
    queries = draw_queries(jax.random.fold_in(seeds[11], 71), 0)
    cand_owner_keys = jax.random.split(jax.random.fold_in(seeds[3], 1), PAIRS // PAIR_C)
    cand_owner_turns = jax.random.permutation(jax.random.fold_in(seeds[3], 3), PAIRS // PAIR_C)
    cand_owner = jax.vmap(lambda own, number: deal_out(jax.random.fold_in(seeds[3], 2), own, number, PAIR_C, N_CORPUS, 1, CAP, 2))(cand_owner_keys, cand_owner_turns).reshape((PAIRS, 1))
    cand_block = plant(jax.random.randint(seeds[4], (PAIRS,), 0, OWN_BLKS), jax.random.fold_in(seeds[4], 1), 0, OWN_BLKS - 1).astype(jnp.int32)
    cand_query = plant(jax.random.randint(seeds[5], (PAIRS,), 0, NQ), jax.random.fold_in(seeds[5], 1), 0, NQ - 1).astype(jnp.int32)
    norm_gain = jnp.clip(1.0 + 0.18 * jax.random.normal(seeds[6], (D,), jnp.float32), 0.099609375, 1.8984375).astype(jnp.bfloat16)
    w_query = draw_w_query(jax.random.fold_in(seeds[11], 71), 0)
    w_key = draw_w_key(jax.random.fold_in(seeds[11], 71), 0)
    w_value = gaussian(seeds[9], (D, KW), D ** -0.5, 0.09375, ((0, 8),))
    w_score = gaussian(seeds[10], (QW,), QW ** -0.5, 0.125)
    return {"store_rows": store_rows, "block_lengths": block_lengths, "queries": queries, "cand_owner": cand_owner, "cand_block": cand_block, "cand_query": cand_query, "norm_gain": norm_gain, "w_query": w_query, "w_key": w_key, "w_value": w_value, "w_score": w_score}


ROPE_BASE = 1000000.0
EPSILON = 1e-06

def rotate(values, positions):
    head_dim = values.shape[-1]
    half_dim = head_dim // 2
    inverse = jnp.power(ROPE_BASE, -2.0 * jnp.arange(half_dim, dtype=jnp.float32) / head_dim)
    angles = positions.astype(jnp.float32)[..., None] * inverse
    cosine = jnp.cos(angles)[..., None, :]
    sine_part = jnp.sin(angles)[..., None, :]
    lower = values[..., :half_dim]
    upper = values[..., half_dim:]
    return jnp.concatenate([lower * cosine - upper * sine_part, upper * cosine + lower * sine_part], axis=-1)

def attend(joined, length, norm_gain, w_query, w_key, w_value, w_score):
    seq_len = joined.shape[0]
    widened = joined.astype(jnp.float32)
    inverse_rms = lax.rsqrt(lax.optimization_barrier(jnp.mean(widened * widened, axis=-1, keepdims=True)) + EPSILON)
    normed = (widened * inverse_rms * norm_gain.astype(jnp.float32)).astype(jnp.bfloat16)
    query_raw = jnp.dot(normed, w_query, preferred_element_type=jnp.float32)
    key_raw = jnp.dot(normed, w_key, preferred_element_type=jnp.float32)
    value_raw = jnp.dot(normed, w_value, preferred_element_type=jnp.float32)
    token_ids = jnp.arange(seq_len, dtype=jnp.int32)
    positions = jnp.where(token_ids < BLK, token_ids, length + token_ids - BLK)
    query_rot = rotate(query_raw.reshape(seq_len, QHEADS, HDIM), positions).astype(jnp.bfloat16)
    key_rot = rotate(key_raw.reshape(seq_len, KVHEADS, HDIM), positions).astype(jnp.bfloat16)
    values = value_raw.reshape(seq_len, KVHEADS, HDIM).astype(jnp.bfloat16)
    grouped = query_rot.reshape(seq_len, KVHEADS, QHEADS // KVHEADS, HDIM)
    logits = jnp.einsum('skgd,tkd->kgst', grouped.astype(jnp.float32), key_rot.astype(jnp.float32)) * HDIM ** (-0.5)
    live = (token_ids < length) | (token_ids >= BLK)
    allowed = live[None, :] & (token_ids[None, :] <= token_ids[:, None])
    masked = jnp.where(allowed, logits, -1e+30)
    peak = lax.optimization_barrier(jnp.max(masked, axis=-1, keepdims=True))
    weights = jnp.where(allowed, jnp.exp(masked - peak), 0.0)
    probs = (weights / lax.optimization_barrier(jnp.sum(weights, axis=-1, keepdims=True))).astype(jnp.bfloat16)
    context = jnp.einsum('kgst,tkd->skgd', probs.astype(jnp.float32), values.astype(jnp.float32))
    context = context.reshape(seq_len, QHEADS * HDIM).astype(jnp.bfloat16)
    score = jnp.dot(context[seq_len - 1], w_score, preferred_element_type=jnp.float32)
    keep = token_ids[:BLK] < length
    passage = jnp.where(keep[:, None], context[:BLK], jnp.zeros((), jnp.bfloat16))
    return (passage, score)

def reference(store_rows, block_lengths, queries, cand_owner, cand_block, cand_query, norm_gain, w_query, w_key, w_value, w_score):
    pair_total = cand_block.shape[0]
    pair_group = pair_total // N_CORPUS
    owners = cand_owner[:, 0]
    pair_order = jnp.arange(pair_total, dtype=jnp.int32)
    group_of = pair_order // pair_group
    earlier = (owners[:, None] == owners[None, :]) & (group_of[:, None] == group_of[None, :]) & (pair_order[None, :] < pair_order[:, None])
    owner_rank = lax.optimization_barrier(jnp.sum(earlier.astype(jnp.int32), axis=1))
    block_of = owners * OWN_BLKS + cand_block

    def run_pair(index):
        block = block_of[index]
        joined = jnp.concatenate([store_rows[block], queries[cand_query[index]]], axis=0)
        return attend(joined, block_lengths[block], norm_gain, w_query, w_key, w_value, w_score)
    passages, pair_scores = lax.map(run_pair, pair_order)
    slot_ids = ((owners * N_CORPUS + group_of) * CAP + owner_rank).astype(jnp.int32)
    passage_context = jnp.zeros((N_CORPUS * N_CORPUS * CAP, BLK, QHEADS * HDIM), jnp.bfloat16).at[slot_ids].set(passages)
    return (passage_context, pair_scores)
```

```python
import functools

import jax
import jax.numpy as jnp
from jax import lax
from jax.experimental import pallas as pl
from jax.experimental.pallas import tpu as pltpu
from jax.sharding import PartitionSpec as P

HDIM = 128
QHEADS = 14
KVHEADS = 2
GROUP = QHEADS // KVHEADS
CAP = 5
LAST_PAD = 8

ROPE_BASE = 1000000.0
EPSILON = 1e-06
NEG = -1e30
VMEM = 56 << 20


def norm_kernel(ids_ref, rows_ref, gain_ref, out_ref):
    del ids_ref
    rows = rows_ref[0].astype(jnp.float32)
    scale = lax.rsqrt(jnp.mean(rows * rows, axis=-1, keepdims=True) + EPSILON)
    out_ref[0] = (rows * scale * gain_ref[...].astype(jnp.float32)).astype(out_ref.dtype)


def pick_and_norm(table, ids, gain):
    count = ids.shape[0]
    _, rows, width = table.shape
    return pl.pallas_call(
        norm_kernel,
        out_shape=jax.ShapeDtypeStruct((count, rows, width), table.dtype),
        grid_spec=pltpu.PrefetchScalarGridSpec(
            num_scalar_prefetch=1,
            grid=(count,),
            in_specs=[
                pl.BlockSpec((1, rows, width), lambda s, ids: (ids[s], 0, 0)),
                pl.BlockSpec((1, width), lambda s, ids: (0, 0)),
            ],
            out_specs=pl.BlockSpec((1, rows, width), lambda s, ids: (s, 0, 0)),
        ),
        cost_estimate=pl.CostEstimate(
            flops=4 * count * rows * width,
            transcendentals=0,
            bytes_accessed=4 * count * rows * width,
        ),
    )(ids, table, gain)


def project_kernel(tile, rotated, x_ref, w_ref, cos_ref, sin_ref, out_ref):
    total = x_ref.shape[0]
    columns = w_ref.shape[1]

    def piece(step, rope):
        rows = pl.ds(pl.multiple_of(step * tile, tile), tile)
        raw = jnp.dot(x_ref[rows, :], w_ref[...], preferred_element_type=jnp.float32)
        if not rope:
            out_ref[rows, :] = raw.astype(out_ref.dtype)
            return
        cosine = cos_ref[rows, :]
        sine = sin_ref[rows, :]
        for head in range(columns // HDIM):
            part = raw[:, head * HDIM : (head + 1) * HDIM]
            turned = part * cosine + pltpu.roll(part, HDIM // 2, 1) * sine
            out_ref[rows, head * HDIM : (head + 1) * HDIM] = turned.astype(out_ref.dtype)

    def run(rope):
        @pl.loop(0, total // tile)
        def _(step):
            piece(step, rope)

    if rotated is None:
        run(True)
    else:

        @pl.when(pl.program_id(0) < rotated)
        def _():
            run(True)

        @pl.when(pl.program_id(0) >= rotated)
        def _():
            run(False)


def project(x, w, cosine, sine, rotated=None):
    rows, depth = x.shape
    columns = w.shape[1]
    block = 2 * HDIM
    tile = max(t for t in range(16, 481, 16) if rows % t == 0)
    return pl.pallas_call(
        functools.partial(project_kernel, tile, rotated),
        out_shape=jax.ShapeDtypeStruct((rows, columns), x.dtype),
        grid=(columns // block,),
        in_specs=[
            pl.BlockSpec((rows, depth), lambda j: (0, 0), pipeline_mode=pl.Buffered(1)),
            pl.BlockSpec((depth, block), lambda j: (0, j)),
            pl.BlockSpec((rows, HDIM), lambda j: (0, 0), pipeline_mode=pl.Buffered(1)),
            pl.BlockSpec((rows, HDIM), lambda j: (0, 0), pipeline_mode=pl.Buffered(1)),
        ],
        out_specs=pl.BlockSpec((rows, block), lambda j: (0, j)),
        compiler_params=pltpu.CompilerParams(vmem_limit_bytes=VMEM),
        cost_estimate=pl.CostEstimate(
            flops=2 * rows * depth * columns,
            transcendentals=0,
            bytes_accessed=2 * (rows * depth + depth * columns + rows * columns),
        ),
    )(x, w, cosine, sine)


def attend_kernel(
    widths, members, len_ref, q_ref, kv_ref, last_ref, ask_ref, wscore_ref, out_ref, score_ref
):
    slot = pl.program_id(0)
    member = lax.axis_index("rerank")
    length = len_ref[slot]
    chunk = q_ref.shape[0]
    start = member * chunk
    live = start < length
    keys = KVHEADS * HDIM
    scale = HDIM ** (-0.5)

    def columns(head):
        return slice(head * HDIM, (head + 1) * HDIM)

    def attend(width):
        rows = GROUP * chunk
        token = start + lax.broadcasted_iota(jnp.int32, (chunk, width), 0)
        allowed = lax.broadcasted_iota(jnp.int32, (chunk, width), 1) <= token
        allowed = jnp.concatenate([allowed.astype(jnp.float32)] * GROUP, axis=0) > 0.5
        keep = start + lax.broadcasted_iota(jnp.int32, (chunk, HDIM), 0) < length
        for head in range(KVHEADS):
            query = jnp.concatenate(
                [q_ref[:, columns(head * GROUP + g)] for g in range(GROUP)], axis=0
            )
            key = kv_ref[: width // chunk, 0, :, columns(head)].reshape(width, HDIM)
            value = kv_ref[
                : width // chunk, 0, :, keys + head * HDIM : keys + (head + 1) * HDIM
            ].reshape(width, HDIM)
            logits = scale * lax.dot_general(
                query, key, (((1,), (1,)), ((), ())), preferred_element_type=jnp.float32
            )
            masked = jnp.where(allowed, logits, NEG)
            weights = jnp.exp(masked - jnp.max(masked, axis=-1, keepdims=True))
            inverse = 1.0 / jnp.sum(weights, axis=-1, keepdims=True)
            probs = (weights * inverse).astype(jnp.bfloat16)
            context = jnp.dot(probs, value, preferred_element_type=jnp.float32)
            for g in range(GROUP):
                part = context[g * chunk : (g + 1) * chunk]
                out_ref[0, :, columns(head * GROUP + g)] = jnp.where(keep, part, 0.0).astype(
                    out_ref.dtype
                )

    @pl.when(jnp.logical_not(live))
    def _():
        out_ref[...] = jnp.zeros_like(out_ref)

    below = 0
    for width in widths:
        end = start + chunk

        @pl.when(live & (end > below) & (end <= width))
        def _(width=width):
            attend(width)

        below = width

    @pl.when(member < members - 1)
    def _():
        score_ref[...] = jnp.zeros_like(score_ref)

    @pl.when(member == members - 1)
    def _():
        tokens = members * chunk
        total = jnp.zeros((LAST_PAD, HDIM), jnp.float32)
        seen = lax.broadcasted_iota(jnp.int32, (LAST_PAD, tokens), 1) < length
        for head in range(KVHEADS):
            query = last_ref[0, head]
            key = kv_ref[:, 0, :, columns(head)].reshape(tokens, HDIM)
            value = kv_ref[:, 0, :, keys + head * HDIM : keys + (head + 1) * HDIM].reshape(
                tokens, HDIM
            )
            ask_key = ask_ref[0, :, columns(head)]
            ask_value = ask_ref[0, :, keys + head * HDIM : keys + (head + 1) * HDIM]
            contract = (((1,), (1,)), ((), ()))
            first = scale * lax.dot_general(
                query, key, contract, preferred_element_type=jnp.float32
            )
            first = jnp.where(seen, first, NEG)
            second = scale * lax.dot_general(
                query, ask_key, contract, preferred_element_type=jnp.float32
            )
            peak = jnp.maximum(
                jnp.max(first, axis=-1, keepdims=True), jnp.max(second, axis=-1, keepdims=True)
            )
            first = jnp.exp(first - peak)
            second = jnp.exp(second - peak)
            inverse = 1.0 / (
                jnp.sum(first, axis=-1, keepdims=True) + jnp.sum(second, axis=-1, keepdims=True)
            )
            context = jnp.dot(
                (first * inverse).astype(jnp.bfloat16), value, preferred_element_type=jnp.float32
            ) + jnp.dot(
                (second * inverse).astype(jnp.bfloat16),
                ask_value,
                preferred_element_type=jnp.float32,
            )
            context = context.astype(jnp.bfloat16).astype(jnp.float32)
            total = total + context * wscore_ref[head].astype(jnp.float32)
        score_ref[0] = total


def attend(lengths, query, gathered, last, asked, w_score):
    slots = lengths.shape[0]
    members, _, chunk, kv_width = gathered.shape
    width = query.shape[1]
    tokens = members * chunk
    asking = asked.shape[1]
    widths = [w for w in (128, 256) if w < tokens and w % chunk == 0] + [tokens]
    fixed = lambda s, n: (0, 0, 0)
    return pl.pallas_call(
        functools.partial(attend_kernel, widths, members),
        out_shape=(
            jax.ShapeDtypeStruct((slots, chunk, width), query.dtype),
            jax.ShapeDtypeStruct((slots, LAST_PAD, HDIM), jnp.float32),
        ),
        grid_spec=pltpu.PrefetchScalarGridSpec(
            num_scalar_prefetch=1,
            grid=(slots,),
            in_specs=[
                pl.BlockSpec((chunk, width), lambda s, n: (s, 0)),
                pl.BlockSpec((members, 1, chunk, kv_width), lambda s, n: (0, s, 0, 0)),
                pl.BlockSpec((1, KVHEADS, LAST_PAD, HDIM), lambda s, n: (s, 0, 0, 0)),
                pl.BlockSpec((1, asking, kv_width), lambda s, n: (s, 0, 0)),
                pl.BlockSpec((KVHEADS, LAST_PAD, HDIM), fixed),
            ],
            out_specs=(
                pl.BlockSpec((1, chunk, width), lambda s, n: (s, 0, 0)),
                pl.BlockSpec((1, LAST_PAD, HDIM), lambda s, n: (s, 0, 0)),
            ),
        ),
        compiler_params=pltpu.CompilerParams(vmem_limit_bytes=VMEM),
        cost_estimate=pl.CostEstimate(
            flops=4 * slots * chunk * tokens * width,
            transcendentals=slots * chunk * QHEADS * tokens,
            bytes_accessed=2 * slots * (2 * chunk * width + tokens * kv_width),
        ),
    )(lengths, query, gathered, last, asked, w_score)


def by_head(values):
    split = values.reshape(values.shape[:-1] + (KVHEADS, GROUP, HDIM))
    pads = [(0, 0)] * (split.ndim - 2) + [(0, LAST_PAD - GROUP), (0, 0)]
    return jnp.pad(split, pads)


def on_device(
    store_rows,
    block_lengths,
    queries,
    cand_owner,
    cand_block,
    cand_query,
    norm_gain,
    w_query,
    w_key,
    w_value,
    w_score,
):
    n_corpus = lax.axis_size("corpus")
    n_rerank = lax.axis_size("rerank")
    corpus_index = lax.axis_index("corpus")
    member = lax.axis_index("rerank")
    w_pair = lax.all_gather(
        jnp.concatenate([w_key, w_value], axis=1), "rerank", axis=0, tiled=True
    )
    w_all = lax.all_gather(w_query, "rerank", axis=0, tiled=True)

    pair_total = cand_block.shape[0]
    pair_group = pair_total // n_corpus
    pair_dev = pair_group // n_rerank
    own_blocks, chunk, depth = store_rows.shape
    asking = queries.shape[1]
    owners = cand_owner[:, 0]
    pair_order = jnp.arange(pair_total, dtype=jnp.int32)
    group_of = pair_order // pair_group
    earlier = (
        (owners[:, None] == owners[None, :])
        & (group_of[:, None] == group_of[None, :])
        & (pair_order[None, :] < pair_order[:, None])
    )
    owner_rank = jnp.sum(earlier.astype(jnp.int32), axis=1)
    slots = n_corpus * CAP
    slot_ids = jnp.arange(slots, dtype=jnp.int32)
    wanted = (owners == corpus_index)[None, :] & (
        (group_of * CAP + owner_rank)[None, :] == slot_ids[:, None]
    )

    def per_slot(values):
        return jnp.sum(jnp.where(wanted, values[None, :], 0), axis=1)

    block_ids = per_slot(cand_block)
    query_ids = per_slot(cand_query)
    own_lengths = lax.dynamic_slice(block_lengths, (corpus_index * own_blocks,), (own_blocks,))
    chosen = block_ids[:, None] == jnp.arange(own_blocks, dtype=jnp.int32)[None, :]
    lengths = jnp.sum(jnp.where(chosen, own_lengths[None, :], 0), axis=1)
    lengths = jnp.where(jnp.any(wanted, axis=1), lengths, 0)

    gain = norm_gain[None, :]
    passages = pick_and_norm(store_rows, block_ids, gain)
    questions = pick_and_norm(queries, query_ids, gain)
    held = slots * chunk
    normed = jnp.concatenate(
        [passages.reshape(held, depth), questions.reshape(slots * asking, depth)], axis=0
    )
    here = jnp.broadcast_to(
        (member * chunk + jnp.arange(chunk, dtype=jnp.int32))[None, :], (slots, chunk)
    )
    there = lengths[:, None] + (member * asking + jnp.arange(asking, dtype=jnp.int32))[None, :]
    positions = jnp.concatenate([here.reshape(-1), there.reshape(-1)])
    half = HDIM // 2
    inverse = jnp.power(ROPE_BASE, -2.0 * jnp.arange(half, dtype=jnp.float32) / HDIM)
    angles = positions.astype(jnp.float32)[:, None] * inverse
    cosine = jnp.cos(angles)
    sine = jnp.sin(angles)
    cosine = jnp.concatenate([cosine, cosine], axis=1)
    sine = jnp.concatenate([-sine, sine], axis=1)

    key_columns = w_key.shape[1]
    pair_out = project(normed, w_pair, cosine, sine, rotated=key_columns // (2 * HDIM))
    gathered = lax.all_gather(pair_out[:held].reshape(slots, chunk, -1), "rerank", axis=0)
    asked = lax.all_gather(pair_out[held:].reshape(slots, asking, -1), "rerank", axis=0)
    asked = jnp.swapaxes(asked, 0, 1).reshape(slots, n_rerank * asking, -1)
    query_out = project(normed, w_all, cosine, sine)
    last = query_out[held:].reshape(slots, asking, -1)[:, asking - 1]
    context, parts = attend(
        lengths, query_out, gathered, by_head(last), asked, by_head(w_score)
    )
    slot_scores = jnp.sum(parts, axis=(1, 2))
    mine = jnp.sum(jnp.where(wanted, slot_scores[:, None], 0.0), axis=0)
    scores = lax.psum(mine, ("corpus", "rerank"))
    first = corpus_index * pair_group + member * pair_dev
    return (context, lax.dynamic_slice(scores, (first,), (pair_dev,)))


def solution(mesh):
    placed = (
        P("corpus", "rerank", None),
        P(),
        P(None, "rerank", None),
        P(),
        P(),
        P(),
        P(),
        P("rerank", None),
        P("rerank", None),
        P("rerank", None),
        P(),
    )
    return jax.shard_map(
        on_device,
        mesh=mesh,
        in_specs=placed,
        out_specs=(P("corpus", "rerank", None), P(("corpus", "rerank"))),
        check_vma=False,
    )
```

```python
import functools

import jax
import jax.numpy as jnp
from jax import lax
from jax.experimental import pallas as pl
from jax.experimental.pallas import tpu as pltpu
from jax.sharding import PartitionSpec as P

HDIM = 128
QHEADS = 14
KVHEADS = 2
GROUP = QHEADS // KVHEADS
CAP = 5
LAST_PAD = 8

ROPE_BASE = 1000000.0
EPSILON = 1e-06
NEG = -1e30
VMEM = 56 << 20


def norm_kernel(ids_ref, rows_ref, gain_ref, out_ref):
    del ids_ref
    rows = rows_ref[0].astype(jnp.float32)
    scale = lax.rsqrt(jnp.mean(rows * rows, axis=-1, keepdims=True) + EPSILON)
    out_ref[0] = (rows * scale * gain_ref[...].astype(jnp.float32)).astype(out_ref.dtype)


def pick_and_norm(table, ids, gain):
    count = ids.shape[0]
    _, rows, width = table.shape
    return pl.pallas_call(
        norm_kernel,
        out_shape=jax.ShapeDtypeStruct((count, rows, width), table.dtype),
        grid_spec=pltpu.PrefetchScalarGridSpec(
            num_scalar_prefetch=1,
            grid=(count,),
            in_specs=[
                pl.BlockSpec((1, rows, width), lambda s, ids: (ids[s], 0, 0)),
                pl.BlockSpec((1, width), lambda s, ids: (0, 0)),
            ],
            out_specs=pl.BlockSpec((1, rows, width), lambda s, ids: (s, 0, 0)),
        ),
        cost_estimate=pl.CostEstimate(
            flops=4 * count * rows * width,
            transcendentals=0,
            bytes_accessed=4 * count * rows * width,
        ),
    )(ids, table, gain)


def project_kernel(tile, rotated, x_ref, w_ref, cos_ref, sin_ref, out_ref):
    total = x_ref.shape[0]
    columns = w_ref.shape[1]

    def piece(step, rope):
        rows = pl.ds(pl.multiple_of(step * tile, tile), tile)
        raw = jnp.dot(x_ref[rows, :], w_ref[...], preferred_element_type=jnp.float32)
        if not rope:
            out_ref[rows, :] = raw.astype(out_ref.dtype)
            return
        cosine = cos_ref[rows, :]
        sine = sin_ref[rows, :]
        for head in range(columns // HDIM):
            part = raw[:, head * HDIM : (head + 1) * HDIM]
            turned = part * cosine + pltpu.roll(part, HDIM // 2, 1) * sine
            out_ref[rows, head * HDIM : (head + 1) * HDIM] = turned.astype(out_ref.dtype)

    def run(rope):
        @pl.loop(0, total // tile)
        def _(step):
            piece(step, rope)

    if rotated is None:
        run(True)
    else:

        @pl.when(pl.program_id(0) < rotated)
        def _():
            run(True)

        @pl.when(pl.program_id(0) >= rotated)
        def _():
            run(False)


def project(x, w, first, columns, cosine, sine, rotated=None):
    rows, depth = x.shape
    block = 2 * HDIM
    skipped = first // block
    tile = max(t for t in range(16, 481, 16) if rows % t == 0)
    return pl.pallas_call(
        functools.partial(project_kernel, tile, rotated),
        out_shape=jax.ShapeDtypeStruct((rows, columns), x.dtype),
        grid=(columns // block,),
        in_specs=[
            pl.BlockSpec((rows, depth), lambda j: (0, 0), pipeline_mode=pl.Buffered(1)),
            pl.BlockSpec((depth, block), lambda j: (0, j + skipped)),
            pl.BlockSpec((rows, HDIM), lambda j: (0, 0), pipeline_mode=pl.Buffered(1)),
            pl.BlockSpec((rows, HDIM), lambda j: (0, 0), pipeline_mode=pl.Buffered(1)),
        ],
        out_specs=pl.BlockSpec((rows, block), lambda j: (0, j)),
        compiler_params=pltpu.CompilerParams(vmem_limit_bytes=VMEM),
        cost_estimate=pl.CostEstimate(
            flops=2 * rows * depth * columns,
            transcendentals=0,
            bytes_accessed=2 * (rows * depth + depth * columns + rows * columns),
        ),
    )(x, w, cosine, sine)


def attend_kernel(
    widths, members, len_ref, q_ref, kv_ref, last_ref, ask_ref, wscore_ref, out_ref, score_ref
):
    slot = pl.program_id(0)
    member = lax.axis_index("rerank")
    length = len_ref[slot]
    chunk = q_ref.shape[0]
    start = member * chunk
    live = start < length
    keys = KVHEADS * HDIM
    scale = HDIM ** (-0.5)

    def columns(head):
        return slice(head * HDIM, (head + 1) * HDIM)

    def attend(width):
        rows = GROUP * chunk
        token = start + lax.broadcasted_iota(jnp.int32, (chunk, width), 0)
        allowed = lax.broadcasted_iota(jnp.int32, (chunk, width), 1) <= token
        allowed = jnp.concatenate([allowed.astype(jnp.float32)] * GROUP, axis=0) > 0.5
        keep = start + lax.broadcasted_iota(jnp.int32, (chunk, HDIM), 0) < length
        for head in range(KVHEADS):
            query = jnp.concatenate(
                [q_ref[:, columns(head * GROUP + g)] for g in range(GROUP)], axis=0
            )
            key = kv_ref[: width // chunk, :, columns(head)].reshape(width, HDIM)
            value = kv_ref[
                : width // chunk, :, keys + head * HDIM : keys + (head + 1) * HDIM
            ].reshape(width, HDIM)
            logits = scale * lax.dot_general(
                query, key, (((1,), (1,)), ((), ())), preferred_element_type=jnp.float32
            )
            masked = jnp.where(allowed, logits, NEG)
            weights = jnp.exp(masked - jnp.max(masked, axis=-1, keepdims=True))
            inverse = 1.0 / jnp.sum(weights, axis=-1, keepdims=True)
            probs = (weights * inverse).astype(jnp.bfloat16)
            context = jnp.dot(probs, value, preferred_element_type=jnp.float32)
            for g in range(GROUP):
                part = context[g * chunk : (g + 1) * chunk]
                out_ref[0, :, columns(head * GROUP + g)] = jnp.where(keep, part, 0.0).astype(
                    out_ref.dtype
                )

    @pl.when(jnp.logical_not(live))
    def _():
        out_ref[...] = jnp.zeros_like(out_ref)

    below = 0
    for width in widths:
        end = start + chunk

        @pl.when(live & (end > below) & (end <= width))
        def _(width=width):
            attend(width)

        below = width

    @pl.when(member < members - 1)
    def _():
        score_ref[...] = jnp.zeros_like(score_ref)

    @pl.when(member == members - 1)
    def _():
        tokens = members * chunk
        total = jnp.zeros((LAST_PAD, HDIM), jnp.float32)
        seen = lax.broadcasted_iota(jnp.int32, (LAST_PAD, tokens), 1) < length
        for head in range(KVHEADS):
            query = last_ref[0, head]
            key = kv_ref[:, :, columns(head)].reshape(tokens, HDIM)
            value = kv_ref[:, :, keys + head * HDIM : keys + (head + 1) * HDIM].reshape(
                tokens, HDIM
            )
            ask_key = ask_ref[0, :, columns(head)]
            ask_value = ask_ref[0, :, keys + head * HDIM : keys + (head + 1) * HDIM]
            contract = (((1,), (1,)), ((), ()))
            first = scale * lax.dot_general(
                query, key, contract, preferred_element_type=jnp.float32
            )
            first = jnp.where(seen, first, NEG)
            second = scale * lax.dot_general(
                query, ask_key, contract, preferred_element_type=jnp.float32
            )
            peak = jnp.maximum(
                jnp.max(first, axis=-1, keepdims=True), jnp.max(second, axis=-1, keepdims=True)
            )
            first = jnp.exp(first - peak)
            second = jnp.exp(second - peak)
            inverse = 1.0 / (
                jnp.sum(first, axis=-1, keepdims=True) + jnp.sum(second, axis=-1, keepdims=True)
            )
            context = jnp.dot(
                (first * inverse).astype(jnp.bfloat16), value, preferred_element_type=jnp.float32
            ) + jnp.dot(
                (second * inverse).astype(jnp.bfloat16),
                ask_value,
                preferred_element_type=jnp.float32,
            )
            context = context.astype(jnp.bfloat16).astype(jnp.float32)
            total = total + context * wscore_ref[head].astype(jnp.float32)
        score_ref[0] = total


def attend(lengths, chunk, query, gathered, last, asked, w_score):
    slots = lengths.shape[0]
    members, _, kv_width = gathered.shape
    width = query.shape[1]
    tokens = members * chunk
    asking = asked.shape[1]
    widths = [w for w in (128, 256) if w < tokens and w % chunk == 0] + [tokens]
    fixed = lambda s, n: (0, 0, 0)
    return pl.pallas_call(
        functools.partial(attend_kernel, widths, members),
        out_shape=(
            jax.ShapeDtypeStruct((slots, chunk, width), query.dtype),
            jax.ShapeDtypeStruct((slots, LAST_PAD, HDIM), jnp.float32),
        ),
        grid_spec=pltpu.PrefetchScalarGridSpec(
            num_scalar_prefetch=1,
            grid=(slots,),
            in_specs=[
                pl.BlockSpec((chunk, width), lambda s, n: (s, 0)),
                pl.BlockSpec((members, chunk, kv_width), lambda s, n: (0, s, 0)),
                pl.BlockSpec((1, KVHEADS, LAST_PAD, HDIM), lambda s, n: (s, 0, 0, 0)),
                pl.BlockSpec((1, asking, kv_width), lambda s, n: (s, 0, 0)),
                pl.BlockSpec((KVHEADS, LAST_PAD, HDIM), fixed),
            ],
            out_specs=(
                pl.BlockSpec((1, chunk, width), lambda s, n: (s, 0, 0)),
                pl.BlockSpec((1, LAST_PAD, HDIM), lambda s, n: (s, 0, 0)),
            ),
        ),
        compiler_params=pltpu.CompilerParams(vmem_limit_bytes=VMEM),
        cost_estimate=pl.CostEstimate(
            flops=4 * slots * chunk * tokens * width,
            transcendentals=slots * chunk * QHEADS * tokens,
            bytes_accessed=2 * slots * (2 * chunk * width + tokens * kv_width),
        ),
    )(lengths, query, gathered, last, asked, w_score)


def by_head(values):
    split = values.reshape(values.shape[:-1] + (KVHEADS, GROUP, HDIM))
    pads = [(0, 0)] * (split.ndim - 2) + [(0, LAST_PAD - GROUP), (0, 0)]
    return jnp.pad(split, pads)


def on_device(
    store_rows,
    block_lengths,
    queries,
    cand_owner,
    cand_block,
    cand_query,
    norm_gain,
    w_query,
    w_key,
    w_value,
    w_score,
):
    n_corpus = lax.axis_size("corpus")
    n_rerank = lax.axis_size("rerank")
    corpus_index = lax.axis_index("corpus")
    member = lax.axis_index("rerank")
    weights = lax.all_gather(
        jnp.concatenate([w_key, w_value, w_query], axis=1), "rerank", axis=0, tiled=True
    )
    pair_columns = w_key.shape[1] + w_value.shape[1]

    pair_total = cand_block.shape[0]
    pair_group = pair_total // n_corpus
    pair_dev = pair_group // n_rerank
    own_blocks, chunk, depth = store_rows.shape
    asking = queries.shape[1]
    owners = cand_owner[:, 0]
    pair_order = jnp.arange(pair_total, dtype=jnp.int32)
    group_of = pair_order // pair_group
    earlier = (
        (owners[:, None] == owners[None, :])
        & (group_of[:, None] == group_of[None, :])
        & (pair_order[None, :] < pair_order[:, None])
    )
    owner_rank = jnp.sum(earlier.astype(jnp.int32), axis=1)
    slots = n_corpus * CAP
    slot_ids = jnp.arange(slots, dtype=jnp.int32)
    wanted = (owners == corpus_index)[None, :] & (
        (group_of * CAP + owner_rank)[None, :] == slot_ids[:, None]
    )

    def per_slot(values):
        return jnp.sum(jnp.where(wanted, values[None, :], 0), axis=1)

    block_ids = per_slot(cand_block)
    query_ids = per_slot(cand_query)
    own_lengths = lax.dynamic_slice(block_lengths, (corpus_index * own_blocks,), (own_blocks,))
    chosen = block_ids[:, None] == jnp.arange(own_blocks, dtype=jnp.int32)[None, :]
    lengths = jnp.sum(jnp.where(chosen, own_lengths[None, :], 0), axis=1)
    lengths = jnp.where(jnp.any(wanted, axis=1), lengths, 0)

    gain = norm_gain[None, :]
    passages = pick_and_norm(store_rows, block_ids, gain)
    questions = pick_and_norm(queries, query_ids, gain)
    held = slots * chunk
    normed = jnp.concatenate(
        [passages.reshape(held, depth), questions.reshape(slots * asking, depth)], axis=0
    )
    here = jnp.broadcast_to(
        (member * chunk + jnp.arange(chunk, dtype=jnp.int32))[None, :], (slots, chunk)
    )
    there = lengths[:, None] + (member * asking + jnp.arange(asking, dtype=jnp.int32))[None, :]
    positions = jnp.concatenate([here.reshape(-1), there.reshape(-1)])
    half = HDIM // 2
    inverse = jnp.power(ROPE_BASE, -2.0 * jnp.arange(half, dtype=jnp.float32) / HDIM)
    angles = positions.astype(jnp.float32)[:, None] * inverse
    cosine = jnp.cos(angles)
    sine = jnp.sin(angles)
    cosine = jnp.concatenate([cosine, cosine], axis=1)
    sine = jnp.concatenate([-sine, sine], axis=1)

    key_columns = w_key.shape[1]
    rotated = key_columns // (2 * HDIM)
    pair_out = project(normed, weights, 0, pair_columns, cosine, sine, rotated)
    gathered = lax.all_gather(pair_out, "rerank", axis=0)
    asked = gathered[:, held:].reshape(n_rerank, slots, asking, pair_columns)
    asked = jnp.swapaxes(asked, 0, 1).reshape(slots, n_rerank * asking, pair_columns)
    query_out = project(normed, weights, pair_columns, w_query.shape[1], cosine, sine)
    last = query_out[held:].reshape(slots, asking, -1)[:, asking - 1]
    context, parts = attend(
        lengths, chunk, query_out, gathered, by_head(last), asked, by_head(w_score)
    )
    slot_scores = jnp.sum(parts, axis=(1, 2))
    mine = jnp.sum(jnp.where(wanted, slot_scores[:, None], 0.0), axis=0)
    pieces = lax.all_to_all(
        mine.reshape(n_corpus * n_rerank, pair_dev),
        ("corpus", "rerank"),
        split_axis=0,
        concat_axis=0,
        tiled=True,
    )
    return (context, jnp.sum(pieces, axis=0))


def solution(mesh):
    placed = (
        P("corpus", "rerank", None),
        P(),
        P(None, "rerank", None),
        P(),
        P(),
        P(),
        P(),
        P("rerank", None),
        P("rerank", None),
        P("rerank", None),
        P(),
    )
    return jax.shard_map(
        on_device,
        mesh=mesh,
        in_specs=placed,
        out_specs=(P("corpus", "rerank", None), P(("corpus", "rerank"))),
        check_vma=False,
    )
```

```python
import functools

import jax
import jax.numpy as jnp
from jax import lax
from jax.experimental import pallas as pl
from jax.experimental.pallas import tpu as pltpu
from jax.sharding import PartitionSpec as P

HDIM = 128
QHEADS = 14
KVHEADS = 2
GROUP = QHEADS // KVHEADS
CAP = 5

ROPE_BASE = 1000000.0
EPSILON = 1e-06
NEG = -1e30
VMEM = 56 << 20


def norm_kernel(ids_ref, rows_ref, gain_ref, out_ref):
    del ids_ref
    rows = rows_ref[0].astype(jnp.float32)
    scale = lax.rsqrt(jnp.mean(rows * rows, axis=-1, keepdims=True) + EPSILON)
    out_ref[0] = (rows * scale * gain_ref[...].astype(jnp.float32)).astype(out_ref.dtype)


def pick_and_norm(table, ids, gain):
    count = ids.shape[0]
    _, rows, width = table.shape
    return pl.pallas_call(
        norm_kernel,
        out_shape=jax.ShapeDtypeStruct((count, rows, width), table.dtype),
        grid_spec=pltpu.PrefetchScalarGridSpec(
            num_scalar_prefetch=1,
            grid=(count,),
            in_specs=[
                pl.BlockSpec((1, rows, width), lambda s, ids: (ids[s], 0, 0)),
                pl.BlockSpec((1, width), lambda s, ids: (0, 0)),
            ],
            out_specs=pl.BlockSpec((1, rows, width), lambda s, ids: (s, 0, 0)),
        ),
        cost_estimate=pl.CostEstimate(
            flops=4 * count * rows * width,
            transcendentals=0,
            bytes_accessed=4 * count * rows * width,
        ),
    )(ids, table, gain)


def project_kernel(tile, rotated, x_ref, w_ref, cos_ref, sin_ref, out_ref):
    total = x_ref.shape[0]
    columns = w_ref.shape[1]

    def piece(step, rope):
        rows = pl.ds(pl.multiple_of(step * tile, tile), tile)
        raw = jnp.dot(x_ref[rows, :], w_ref[...], preferred_element_type=jnp.float32)
        if not rope:
            out_ref[rows, :] = raw.astype(out_ref.dtype)
            return
        cosine = cos_ref[rows, :]
        sine = sin_ref[rows, :]
        for head in range(columns // HDIM):
            part = raw[:, head * HDIM : (head + 1) * HDIM]
            turned = part * cosine + pltpu.roll(part, HDIM // 2, 1) * sine
            out_ref[rows, head * HDIM : (head + 1) * HDIM] = turned.astype(out_ref.dtype)

    def run(rope):
        @pl.loop(0, total // tile)
        def _(step):
            piece(step, rope)

    if rotated is None:
        run(True)
    else:

        @pl.when(pl.program_id(0) < rotated)
        def _():
            run(True)

        @pl.when(pl.program_id(0) >= rotated)
        def _():
            run(False)


def project(x, rows, w, first, columns, cosine, sine, rotated=None):
    depth = x.shape[1]
    block = 2 * HDIM
    skipped = first // block
    tile = max(t for t in range(16, 481, 16) if rows % t == 0)
    return pl.pallas_call(
        functools.partial(project_kernel, tile, rotated),
        out_shape=jax.ShapeDtypeStruct((rows, columns), x.dtype),
        grid=(columns // block,),
        in_specs=[
            pl.BlockSpec((rows, depth), lambda j: (0, 0), pipeline_mode=pl.Buffered(1)),
            pl.BlockSpec((depth, block), lambda j: (0, j + skipped)),
            pl.BlockSpec((rows, HDIM), lambda j: (0, 0), pipeline_mode=pl.Buffered(1)),
            pl.BlockSpec((rows, HDIM), lambda j: (0, 0), pipeline_mode=pl.Buffered(1)),
        ],
        out_specs=pl.BlockSpec((rows, block), lambda j: (0, j)),
        compiler_params=pltpu.CompilerParams(vmem_limit_bytes=VMEM),
        cost_estimate=pl.CostEstimate(
            flops=2 * rows * depth * columns,
            transcendentals=0,
            bytes_accessed=2 * (rows * depth + depth * columns + rows * columns),
        ),
    )(x, w, cosine, sine)


def attend_kernel(
    widths, len_ref, q_ref, kv_ref, out_ref
):
    slot = pl.program_id(0)
    member = lax.axis_index("rerank")
    length = len_ref[slot]
    chunk = q_ref.shape[0]
    start = member * chunk
    live = start < length
    keys = KVHEADS * HDIM
    scale = HDIM ** (-0.5)

    def columns(head):
        return slice(head * HDIM, (head + 1) * HDIM)

    def attend(width):
        rows = GROUP * chunk
        token = start + lax.broadcasted_iota(jnp.int32, (chunk, width), 0)
        allowed = lax.broadcasted_iota(jnp.int32, (chunk, width), 1) <= token
        allowed = jnp.concatenate([allowed.astype(jnp.float32)] * GROUP, axis=0) > 0.5
        keep = start + lax.broadcasted_iota(jnp.int32, (chunk, HDIM), 0) < length
        for head in range(KVHEADS):
            query = jnp.concatenate(
                [q_ref[:, columns(head * GROUP + g)] for g in range(GROUP)], axis=0
            )
            key = kv_ref[: width // chunk, :, columns(head)].reshape(width, HDIM)
            value = kv_ref[
                : width // chunk, :, keys + head * HDIM : keys + (head + 1) * HDIM
            ].reshape(width, HDIM)
            logits = scale * lax.dot_general(
                query, key, (((1,), (1,)), ((), ())), preferred_element_type=jnp.float32
            )
            masked = jnp.where(allowed, logits, NEG)
            weights = jnp.exp(masked - jnp.max(masked, axis=-1, keepdims=True))
            inverse = 1.0 / jnp.sum(weights, axis=-1, keepdims=True)
            probs = (weights * inverse).astype(jnp.bfloat16)
            context = jnp.dot(probs, value, preferred_element_type=jnp.float32)
            for g in range(GROUP):
                part = context[g * chunk : (g + 1) * chunk]
                out_ref[0, :, columns(head * GROUP + g)] = jnp.where(keep, part, 0.0).astype(
                    out_ref.dtype
                )

    @pl.when(jnp.logical_not(live))
    def _():
        out_ref[...] = jnp.zeros_like(out_ref)

    below = 0
    for width in widths:
        end = start + chunk

        @pl.when(live & (end > below) & (end <= width))
        def _(width=width):
            attend(width)

        below = width


def attend(lengths, chunk, query, gathered):
    slots = lengths.shape[0]
    members, _, kv_width = gathered.shape
    width = query.shape[1]
    tokens = members * chunk
    widths = [w for w in (128, 256) if w < tokens and w % chunk == 0] + [tokens]
    return pl.pallas_call(
        functools.partial(attend_kernel, widths),
        out_shape=jax.ShapeDtypeStruct((slots, chunk, width), query.dtype),
        grid_spec=pltpu.PrefetchScalarGridSpec(
            num_scalar_prefetch=1,
            grid=(slots,),
            in_specs=[
                pl.BlockSpec((chunk, width), lambda s, n: (s, 0)),
                pl.BlockSpec((members, chunk, kv_width), lambda s, n: (0, s, 0)),
            ],
            out_specs=pl.BlockSpec((1, chunk, width), lambda s, n: (s, 0, 0)),
        ),
        compiler_params=pltpu.CompilerParams(vmem_limit_bytes=VMEM),
        cost_estimate=pl.CostEstimate(
            flops=4 * slots * chunk * tokens * width,
            transcendentals=slots * chunk * QHEADS * tokens,
            bytes_accessed=2 * slots * (2 * chunk * width + tokens * kv_width),
        ),
    )(lengths, query, gathered)


def from_last(values, axis):
    members = lax.axis_size(axis)
    member = lax.axis_index(axis)
    reach = 1
    while reach < members:
        chain = [(i, i - reach) for i in range(max(members - reach, reach), members)]
        passed = lax.ppermute(values, axis, chain)
        values = jnp.where(member >= members - reach, values, passed)
        reach *= 2
    return values


def last_token(query, passage, question, alive, w_score):
    slots = query.shape[0]
    heads = query.reshape(slots, KVHEADS, GROUP, HDIM)
    both = jnp.concatenate([passage, question], axis=1)
    both = both.reshape(slots, both.shape[1], 2, KVHEADS, HDIM)
    logits = jnp.einsum(
        "skgd,stkd->skgt", heads, both[:, :, 0], preferred_element_type=jnp.float32
    ) * HDIM ** (-0.5)
    masked = jnp.where(alive[:, None, None, :], logits, NEG)
    peak = jnp.max(masked, axis=-1)
    weights = jnp.exp(masked - peak[..., None])
    total = jnp.sum(weights, axis=-1)
    context = jnp.einsum(
        "skgt,stkd->skgd",
        weights.astype(jnp.bfloat16),
        both[:, :, 1],
        preferred_element_type=jnp.float32,
    )
    gains = w_score.astype(jnp.float32).reshape(KVHEADS, GROUP, HDIM)
    part = jnp.sum(context * gains[None], axis=-1)
    return tuple(v.reshape(slots, QHEADS) for v in (peak, total, part))


def on_device(
    store_rows,
    block_lengths,
    queries,
    cand_owner,
    cand_block,
    cand_query,
    norm_gain,
    w_query,
    w_key,
    w_value,
    w_score,
):
    n_corpus = lax.axis_size("corpus")
    n_rerank = lax.axis_size("rerank")
    corpus_index = lax.axis_index("corpus")
    member = lax.axis_index("rerank")
    weights = lax.all_gather(
        jnp.concatenate([w_key, w_value, w_query], axis=1), "rerank", axis=0, tiled=True
    )
    pair_columns = w_key.shape[1] + w_value.shape[1]

    pair_total = cand_block.shape[0]
    pair_group = pair_total // n_corpus
    pair_dev = pair_group // n_rerank
    own_blocks, chunk, depth = store_rows.shape
    asking = queries.shape[1]
    owners = cand_owner[:, 0]
    pair_order = jnp.arange(pair_total, dtype=jnp.int32)
    group_of = pair_order // pair_group
    earlier = (
        (owners[:, None] == owners[None, :])
        & (group_of[:, None] == group_of[None, :])
        & (pair_order[None, :] < pair_order[:, None])
    )
    owner_rank = jnp.sum(earlier.astype(jnp.int32), axis=1)
    slots = n_corpus * CAP
    slot_ids = jnp.arange(slots, dtype=jnp.int32)
    wanted = (owners == corpus_index)[None, :] & (
        (group_of * CAP + owner_rank)[None, :] == slot_ids[:, None]
    )

    def per_slot(values):
        return jnp.sum(jnp.where(wanted, values[None, :], 0), axis=1)

    block_ids = per_slot(cand_block)
    query_ids = per_slot(cand_query)
    own_lengths = lax.dynamic_slice(block_lengths, (corpus_index * own_blocks,), (own_blocks,))
    chosen = block_ids[:, None] == jnp.arange(own_blocks, dtype=jnp.int32)[None, :]
    lengths = jnp.sum(jnp.where(chosen, own_lengths[None, :], 0), axis=1)
    lengths = jnp.where(jnp.any(wanted, axis=1), lengths, 0)

    gain = norm_gain[None, :]
    passages = pick_and_norm(store_rows, block_ids, gain)
    questions = pick_and_norm(queries, query_ids, gain)
    held = slots * chunk
    tail = from_last(queries[:, asking - 1], "rerank")
    tail = jnp.take(tail, query_ids, axis=0).astype(jnp.float32)
    scale = lax.rsqrt(jnp.mean(tail * tail, axis=-1, keepdims=True) + EPSILON)
    tail = (tail * scale * gain.astype(jnp.float32)).astype(jnp.bfloat16)
    tail_rows = pl.cdiv(slots, 16) * 16
    tail = jnp.pad(tail, ((0, tail_rows - slots), (0, 0)))
    ends = jnp.pad(lengths + (n_rerank * asking - 1), (0, tail_rows - slots))
    normed = jnp.concatenate(
        [passages.reshape(held, depth), questions.reshape(slots * asking, depth)], axis=0
    )
    here = jnp.broadcast_to(
        (member * chunk + jnp.arange(chunk, dtype=jnp.int32))[None, :], (slots, chunk)
    )
    there = lengths[:, None] + (member * asking + jnp.arange(asking, dtype=jnp.int32))[None, :]
    positions = jnp.concatenate([here.reshape(-1), there.reshape(-1), ends])
    half = HDIM // 2
    inverse = jnp.power(ROPE_BASE, -2.0 * jnp.arange(half, dtype=jnp.float32) / HDIM)
    angles = positions.astype(jnp.float32)[:, None] * inverse
    cosine = jnp.cos(angles)
    sine = jnp.sin(angles)
    cosine = jnp.concatenate([cosine, cosine], axis=1)
    sine = jnp.concatenate([-sine, sine], axis=1)

    key_columns = w_key.shape[1]
    rotated = key_columns // (2 * HDIM)
    normed, tail = lax.optimization_barrier((normed, tail))
    rows = held + slots * asking
    pair_out = project(normed, rows, weights, 0, pair_columns, cosine, sine, rotated)
    gathered = lax.all_gather(pair_out[:held], "rerank", axis=0)
    wide = w_query.shape[1]
    query_out = project(normed, held, weights, pair_columns, wide, cosine, sine)
    tail_out = project(
        tail, tail_rows, weights, pair_columns, wide, cosine[rows:], sine[rows:]
    )
    seen = (member * chunk + jnp.arange(chunk, dtype=jnp.int32))[None, :] < lengths[:, None]
    alive = jnp.concatenate([seen, jnp.ones((slots, asking), jnp.bool_)], axis=1)
    peak, total, part = last_token(
        tail_out[:slots],
        pair_out[:held].reshape(slots, chunk, pair_columns),
        pair_out[held:].reshape(slots, asking, pair_columns),
        alive,
        w_score,
    )

    def per_pair(values, absent):
        picked = jnp.sum(jnp.where(wanted[:, :, None], values[:, None, :], 0.0), axis=0)
        return jnp.where((owners == corpus_index)[:, None], picked, absent)

    mine = jnp.concatenate(
        [per_pair(peak, NEG), per_pair(total, 0.0), per_pair(part, 0.0)], axis=1
    )
    sources = n_corpus * n_rerank
    pieces = lax.all_to_all(
        mine.reshape(sources, pair_dev * 3 * QHEADS),
        ("corpus", "rerank"),
        split_axis=0,
        concat_axis=0,
        tiled=True,
    ).reshape(sources, pair_dev, 3, QHEADS)
    peak, total, part = pieces[:, :, 0], pieces[:, :, 1], pieces[:, :, 2]
    share = jnp.exp(peak - jnp.max(peak, axis=0, keepdims=True))
    ratio = jnp.sum(share * part, axis=0) / jnp.sum(share * total, axis=0)
    scores = jnp.sum(ratio, axis=-1)
    query_out, scores = lax.optimization_barrier((query_out, scores))
    context = attend(lengths, chunk, query_out, gathered)
    return (context, scores)


def solution(mesh):
    placed = (
        P("corpus", "rerank", None),
        P(),
        P(None, "rerank", None),
        P(),
        P(),
        P(),
        P(),
        P("rerank", None),
        P("rerank", None),
        P("rerank", None),
        P(),
    )
    return jax.shard_map(
        on_device,
        mesh=mesh,
        in_specs=placed,
        out_specs=(P("corpus", "rerank", None), P(("corpus", "rerank"))),
        check_vma=False,
    )
```

```python
import functools

import jax
import jax.numpy as jnp
from jax import lax
from jax.experimental import pallas as pl
from jax.experimental.pallas import tpu as pltpu
from jax.sharding import PartitionSpec as P

HDIM = 128
QHEADS = 14
KVHEADS = 2
GROUP = QHEADS // KVHEADS
CAP = 5

ROPE_BASE = 1000000.0
EPSILON = 1e-06
NEG = -1e30
VMEM = 56 << 20


def norm_kernel(ids_ref, rows_ref, gain_ref, out_ref):
    del ids_ref
    rows = rows_ref[0].astype(jnp.float32)
    scale = lax.rsqrt(jnp.mean(rows * rows, axis=-1, keepdims=True) + EPSILON)
    out_ref[0] = (rows * scale * gain_ref[...].astype(jnp.float32)).astype(out_ref.dtype)


def pick_and_norm(table, ids, gain):
    count = ids.shape[0]
    _, rows, width = table.shape
    return pl.pallas_call(
        norm_kernel,
        out_shape=jax.ShapeDtypeStruct((count, rows, width), table.dtype),
        grid_spec=pltpu.PrefetchScalarGridSpec(
            num_scalar_prefetch=1,
            grid=(count,),
            in_specs=[
                pl.BlockSpec((1, rows, width), lambda s, ids: (ids[s], 0, 0)),
                pl.BlockSpec((1, width), lambda s, ids: (0, 0)),
            ],
            out_specs=pl.BlockSpec((1, rows, width), lambda s, ids: (s, 0, 0)),
        ),
        cost_estimate=pl.CostEstimate(
            flops=4 * count * rows * width,
            transcendentals=0,
            bytes_accessed=4 * count * rows * width,
        ),
    )(ids, table, gain)


def project_kernel(tile, rotated, x_ref, w_ref, cos_ref, sin_ref, out_ref):
    total = x_ref.shape[0]
    columns = w_ref.shape[1]

    def piece(step, rope):
        rows = pl.ds(pl.multiple_of(step * tile, tile), tile)
        raw = jnp.dot(x_ref[rows, :], w_ref[...], preferred_element_type=jnp.float32)
        if not rope:
            out_ref[rows, :] = raw.astype(out_ref.dtype)
            return
        cosine = cos_ref[rows, :]
        sine = sin_ref[rows, :]
        for head in range(columns // HDIM):
            part = raw[:, head * HDIM : (head + 1) * HDIM]
            turned = part * cosine + pltpu.roll(part, HDIM // 2, 1) * sine
            out_ref[rows, head * HDIM : (head + 1) * HDIM] = turned.astype(out_ref.dtype)

    def run(rope):
        @pl.loop(0, total // tile)
        def _(step):
            piece(step, rope)

    if rotated is None:
        run(True)
    else:

        @pl.when(pl.program_id(0) < rotated)
        def _():
            run(True)

        @pl.when(pl.program_id(0) >= rotated)
        def _():
            run(False)


def project(x, rows, w, first, columns, cosine, sine, rotated=None):
    depth = x.shape[1]
    block = 2 * HDIM
    skipped = first // block
    tile = max(t for t in range(16, 481, 16) if rows % t == 0)
    return pl.pallas_call(
        functools.partial(project_kernel, tile, rotated),
        out_shape=jax.ShapeDtypeStruct((rows, columns), x.dtype),
        grid=(columns // block,),
        in_specs=[
            pl.BlockSpec((rows, depth), lambda j: (0, 0), pipeline_mode=pl.Buffered(1)),
            pl.BlockSpec((depth, block), lambda j: (0, j + skipped)),
            pl.BlockSpec((rows, HDIM), lambda j: (0, 0), pipeline_mode=pl.Buffered(1)),
            pl.BlockSpec((rows, HDIM), lambda j: (0, 0), pipeline_mode=pl.Buffered(1)),
        ],
        out_specs=pl.BlockSpec((rows, block), lambda j: (0, j)),
        compiler_params=pltpu.CompilerParams(vmem_limit_bytes=VMEM),
        cost_estimate=pl.CostEstimate(
            flops=2 * rows * depth * columns,
            transcendentals=0,
            bytes_accessed=2 * (rows * depth + depth * columns + rows * columns),
        ),
    )(x, w, cosine, sine)


def attend_kernel(
    widths, len_ref, q_ref, kv_ref, out_ref
):
    slot = pl.program_id(0)
    member = lax.axis_index("rerank")
    length = len_ref[slot]
    chunk = q_ref.shape[0]
    start = member * chunk
    live = start < length
    keys = KVHEADS * HDIM
    scale = HDIM ** (-0.5)

    def columns(head):
        return slice(head * HDIM, (head + 1) * HDIM)

    def attend(width):
        rows = GROUP * chunk
        token = start + lax.broadcasted_iota(jnp.int32, (chunk, width), 0)
        allowed = lax.broadcasted_iota(jnp.int32, (chunk, width), 1) <= token
        allowed = jnp.concatenate([allowed.astype(jnp.float32)] * GROUP, axis=0) > 0.5
        keep = start + lax.broadcasted_iota(jnp.int32, (chunk, HDIM), 0) < length
        for head in range(KVHEADS):
            query = jnp.concatenate(
                [q_ref[:, columns(head * GROUP + g)] for g in range(GROUP)], axis=0
            )
            key = kv_ref[: width // chunk, :, columns(head)].reshape(width, HDIM)
            value = kv_ref[
                : width // chunk, :, keys + head * HDIM : keys + (head + 1) * HDIM
            ].reshape(width, HDIM)
            logits = scale * lax.dot_general(
                query, key, (((1,), (1,)), ((), ())), preferred_element_type=jnp.float32
            )
            masked = jnp.where(allowed, logits, NEG)
            weights = jnp.exp(masked - jnp.max(masked, axis=-1, keepdims=True))
            inverse = 1.0 / jnp.sum(weights, axis=-1, keepdims=True)
            probs = (weights * inverse).astype(jnp.bfloat16)
            context = jnp.dot(probs, value, preferred_element_type=jnp.float32)
            for g in range(GROUP):
                part = context[g * chunk : (g + 1) * chunk]
                out_ref[0, :, columns(head * GROUP + g)] = jnp.where(keep, part, 0.0).astype(
                    out_ref.dtype
                )

    @pl.when(jnp.logical_not(live))
    def _():
        out_ref[...] = jnp.zeros_like(out_ref)

    below = 0
    for width in widths:
        end = start + chunk

        @pl.when(live & (end > below) & (end <= width))
        def _(width=width):
            attend(width)

        below = width


def attend(lengths, chunk, query, gathered):
    slots = lengths.shape[0]
    members, _, kv_width = gathered.shape
    width = query.shape[1]
    tokens = members * chunk
    widths = [w for w in (128, 256) if w < tokens and w % chunk == 0] + [tokens]
    return pl.pallas_call(
        functools.partial(attend_kernel, widths),
        out_shape=jax.ShapeDtypeStruct((slots, chunk, width), query.dtype),
        grid_spec=pltpu.PrefetchScalarGridSpec(
            num_scalar_prefetch=1,
            grid=(slots,),
            in_specs=[
                pl.BlockSpec((chunk, width), lambda s, n: (s, 0)),
                pl.BlockSpec((members, chunk, kv_width), lambda s, n: (0, s, 0)),
            ],
            out_specs=pl.BlockSpec((1, chunk, width), lambda s, n: (s, 0, 0)),
        ),
        compiler_params=pltpu.CompilerParams(vmem_limit_bytes=VMEM),
        cost_estimate=pl.CostEstimate(
            flops=4 * slots * chunk * tokens * width,
            transcendentals=slots * chunk * QHEADS * tokens,
            bytes_accessed=2 * slots * (2 * chunk * width + tokens * kv_width),
        ),
    )(lengths, query, gathered)


def from_last(values, axis):
    members = lax.axis_size(axis)
    member = lax.axis_index(axis)
    reach = 1
    while reach < members:
        chain = [(i, i - reach) for i in range(max(members - reach, reach), members)]
        passed = lax.ppermute(values, axis, chain)
        values = jnp.where(member >= members - reach, values, passed)
        reach *= 2
    return values


def last_token(query, passage, question, alive, w_score):
    slots = query.shape[0]
    heads = query.reshape(slots, KVHEADS, GROUP, HDIM)
    both = jnp.concatenate([passage, question], axis=1)
    both = both.reshape(slots, both.shape[1], 2, KVHEADS, HDIM)
    logits = jnp.einsum(
        "skgd,stkd->skgt", heads, both[:, :, 0], preferred_element_type=jnp.float32
    ) * HDIM ** (-0.5)
    masked = jnp.where(alive[:, None, None, :], logits, NEG)
    peak = jnp.max(masked, axis=-1)
    weights = jnp.exp(masked - peak[..., None])
    total = jnp.sum(weights, axis=-1)
    context = jnp.einsum(
        "skgt,stkd->skgd",
        weights.astype(jnp.bfloat16),
        both[:, :, 1],
        preferred_element_type=jnp.float32,
    )
    gains = w_score.astype(jnp.float32).reshape(KVHEADS, GROUP, HDIM)
    part = jnp.sum(context * gains[None], axis=-1)
    return tuple(v.reshape(slots, QHEADS) for v in (peak, total, part))


def on_device(
    store_rows,
    block_lengths,
    queries,
    cand_owner,
    cand_block,
    cand_query,
    norm_gain,
    w_query,
    w_key,
    w_value,
    w_score,
):
    n_corpus = lax.axis_size("corpus")
    n_rerank = lax.axis_size("rerank")
    corpus_index = lax.axis_index("corpus")
    member = lax.axis_index("rerank")
    weights = lax.all_gather(
        jnp.concatenate([w_key, w_value, w_query], axis=1), "rerank", axis=0, tiled=True
    )
    pair_columns = w_key.shape[1] + w_value.shape[1]

    pair_total = cand_block.shape[0]
    pair_group = pair_total // n_corpus
    pair_dev = pair_group // n_rerank
    own_blocks, chunk, depth = store_rows.shape
    asking = queries.shape[1]
    owners = cand_owner[:, 0]
    pair_order = jnp.arange(pair_total, dtype=jnp.int32)
    group_of = pair_order // pair_group
    earlier = (
        (owners[:, None] == owners[None, :])
        & (group_of[:, None] == group_of[None, :])
        & (pair_order[None, :] < pair_order[:, None])
    )
    owner_rank = jnp.sum(earlier.astype(jnp.int32), axis=1)
    slots = n_corpus * CAP
    slot_ids = jnp.arange(slots, dtype=jnp.int32)
    wanted = (owners == corpus_index)[None, :] & (
        (group_of * CAP + owner_rank)[None, :] == slot_ids[:, None]
    )

    def per_slot(values):
        return jnp.sum(jnp.where(wanted, values[None, :], 0), axis=1)

    block_ids = per_slot(cand_block)
    query_ids = per_slot(cand_query)
    own_lengths = lax.dynamic_slice(block_lengths, (corpus_index * own_blocks,), (own_blocks,))
    chosen = block_ids[:, None] == jnp.arange(own_blocks, dtype=jnp.int32)[None, :]
    lengths = jnp.sum(jnp.where(chosen, own_lengths[None, :], 0), axis=1)
    lengths = jnp.where(jnp.any(wanted, axis=1), lengths, 0)

    gain = norm_gain[None, :]
    passages = pick_and_norm(store_rows, block_ids, gain)
    questions = pick_and_norm(queries, query_ids, gain)
    held = slots * chunk
    tail = from_last(queries[:, asking - 1], "rerank")
    tail = jnp.take(tail, query_ids, axis=0).astype(jnp.float32)
    scale = lax.rsqrt(jnp.mean(tail * tail, axis=-1, keepdims=True) + EPSILON)
    tail = (tail * scale * gain.astype(jnp.float32)).astype(jnp.bfloat16)
    tail_rows = pl.cdiv(slots, 16) * 16
    tail = jnp.pad(tail, ((0, tail_rows - slots), (0, 0)))
    ends = jnp.pad(lengths + (n_rerank * asking - 1), (0, tail_rows - slots))
    normed = passages.reshape(held, depth)
    questions = questions.reshape(slots * asking, depth)
    here = jnp.broadcast_to(
        (member * chunk + jnp.arange(chunk, dtype=jnp.int32))[None, :], (slots, chunk)
    )
    there = lengths[:, None] + (member * asking + jnp.arange(asking, dtype=jnp.int32))[None, :]
    positions = jnp.concatenate([here.reshape(-1), there.reshape(-1), ends])
    half = HDIM // 2
    inverse = jnp.power(ROPE_BASE, -2.0 * jnp.arange(half, dtype=jnp.float32) / HDIM)
    angles = positions.astype(jnp.float32)[:, None] * inverse
    cosine = jnp.cos(angles)
    sine = jnp.sin(angles)
    cosine = jnp.concatenate([cosine, cosine], axis=1)
    sine = jnp.concatenate([-sine, sine], axis=1)

    key_columns = w_key.shape[1]
    rotated = key_columns // (2 * HDIM)
    normed, questions, tail = lax.optimization_barrier((normed, questions, tail))
    rows = held + slots * asking
    pair_out = project(normed, held, weights, 0, pair_columns, cosine, sine, rotated)
    gathered = lax.all_gather(pair_out, "rerank", axis=0)
    ask_out = project(
        questions,
        slots * asking,
        weights,
        0,
        pair_columns,
        cosine[held:rows],
        sine[held:rows],
        rotated,
    )
    wide = w_query.shape[1]
    query_out = project(normed, held, weights, pair_columns, wide, cosine, sine)
    tail_out = project(
        tail, tail_rows, weights, pair_columns, wide, cosine[rows:], sine[rows:]
    )
    seen = (member * chunk + jnp.arange(chunk, dtype=jnp.int32))[None, :] < lengths[:, None]
    alive = jnp.concatenate([seen, jnp.ones((slots, asking), jnp.bool_)], axis=1)
    peak, total, part = last_token(
        tail_out[:slots],
        pair_out.reshape(slots, chunk, pair_columns),
        ask_out.reshape(slots, asking, pair_columns),
        alive,
        w_score,
    )

    def per_pair(values, absent):
        picked = jnp.sum(jnp.where(wanted[:, :, None], values[:, None, :], 0.0), axis=0)
        return jnp.where((owners == corpus_index)[:, None], picked, absent)

    mine = jnp.concatenate(
        [per_pair(peak, NEG), per_pair(total, 0.0), per_pair(part, 0.0)], axis=1
    )
    sources = n_corpus * n_rerank
    pieces = lax.all_to_all(
        mine.reshape(sources, pair_dev * 3 * QHEADS),
        ("corpus", "rerank"),
        split_axis=0,
        concat_axis=0,
        tiled=True,
    ).reshape(sources, pair_dev, 3, QHEADS)
    peak, total, part = pieces[:, :, 0], pieces[:, :, 1], pieces[:, :, 2]
    share = jnp.exp(peak - jnp.max(peak, axis=0, keepdims=True))
    ratio = jnp.sum(share * part, axis=0) / jnp.sum(share * total, axis=0)
    scores = jnp.sum(ratio, axis=-1)
    query_out, scores = lax.optimization_barrier((query_out, scores))
    context = attend(lengths, chunk, query_out, gathered)
    return (context, scores)


def solution(mesh):
    placed = (
        P("corpus", "rerank", None),
        P(),
        P(None, "rerank", None),
        P(),
        P(),
        P(),
        P(),
        P("rerank", None),
        P("rerank", None),
        P("rerank", None),
        P(),
    )
    return jax.shard_map(
        on_device,
        mesh=mesh,
        in_specs=placed,
        out_specs=(P("corpus", "rerank", None), P(("corpus", "rerank"))),
        check_vma=False,
    )
```
